32 devices in a mesh: rep: 4 (over z), row: 4 (over y, core), col: 2 (over x).
Axes of the slice: x: 2, y: 2, z: 4, core: 2. Of those that a mesh axis runs over, the one named last changes fastest.
Arguments:
- weights: bfloat16 [4, 4096, 2048], P('rep', 'row', 'col'), may hold values from -3 to 3
- tracker: bfloat16 [4, 4096, 2048], P('rep', 'row', 'col'), may hold values from -6 to 6
- grad_prev: bfloat16 [4, 4096, 2048], P('rep', 'row', 'col'), may hold values from -6 to 6
- pool: bfloat16 [4, 1024, 2048], P('rep', 'row', 'col'), may hold values from -6 to 6
- out_grads: bfloat16 [4, 2, 512, 4096], P('rep', None, 'col', 'row'), may hold values from -0.25 to 0.25
- row_ids: int32 [4, 2, 512], P('rep'), may hold values from 0 to 1023
- step_index: int32 [1], replicated, may hold values from 0 to 999
Outputs:
- new_weights: bfloat16 [4, 4096, 2048], P('rep', 'row', 'col')
- new_tracker: bfloat16 [4, 4096, 2048], P('rep', 'row', 'col')
The draws below stay inside these ranges and needn't reach their ends.
Inputs may be any that keep to these rules, and one draw needn't show every extreme that they name: `row_ids`: rows may repeat and need not all be used.
All inputs are finite; a program needn't handle non-finite values.
Results may differ from the reference program's by a relative error of at most 0.0085.
Values may be sent and summed in bfloat16 or wider, within the bound.
No kernel may reach another device: no remote copies, remote signals or barrier semaphores. Data moves between devices by JAX's collectives and lax.ppermute only.
A program may use at most 128 MiB of HBM per device.

```python
import math
import jax
import jax.numpy as jnp
from jax import lax

D = 2048
QOUT = 4096
GRID = 4
NS_ITERS = 2
STEPS = 2
REPS = 4
BATCH = 512
POOL = 1024


def plant(drawn, own_key, smallest, largest):
    place = [jax.random.randint(jax.random.fold_in(own_key, axis), (), 0, length) for axis, length in enumerate(drawn.shape)]
    longest = drawn.shape.index(max(drawn.shape))
    next_to = place[:longest] + [(place[longest] + 1) % drawn.shape[longest]] + place[longest + 1:]
    return drawn.at[tuple(place)].set(smallest).at[tuple(next_to)].set(largest)


def block_scale(key, dims, shards, low, top_value):
    gain = 1.0
    for dim, parts in shards:
        draws = jax.random.uniform(jax.random.fold_in(jax.random.fold_in(key, 6), dim), (parts,), jnp.float32, low / len(shards), top_value / len(shards))
        gain = gain * jnp.repeat(jnp.exp(draws), dims[dim] // parts).reshape((-1,) + (1,) * (len(dims) - 1 - dim))
    return gain


def centred(key, shape, deviation, reach, cuts=(), kind=jnp.bfloat16):
    factor_of = block_scale(key, shape, cuts, -0.22, 0.18) if cuts else 1.0
    drawn = jax.random.normal(key, shape, jnp.float32) * deviation * factor_of
    return jnp.minimum(jnp.maximum(drawn, -reach), reach).astype(kind)


def setup_inputs(seed: int = 0) -> dict:
    seeds = jax.random.split(jax.random.key(seed), 8)
    return {
        "weights": centred(seeds[0], (REPS, QOUT, D), 0.5, 3.0, ((0, 4), (1, 4), (2, 2))),
        "tracker": centred(seeds[1], (REPS, QOUT, D), 1.0, 6.0, ((0, 4), (1, 4), (2, 2))),
        "grad_prev": centred(seeds[2], (REPS, QOUT, D), 1.0, 6.0, ((0, 4), (1, 4), (2, 2))),
        "pool": centred(seeds[3], (REPS, POOL, D), 1.0, 6.0, ((0, 4), (1, 4), (2, 2))),
        "out_grads": centred(seeds[4], (REPS, STEPS, BATCH, QOUT), BATCH ** -0.5, 0.25, ((0, 4), (2, 2), (3, 4))),
        "row_ids": plant(jax.random.randint(seeds[5], (REPS, STEPS, BATCH), 0, POOL), jax.random.fold_in(seeds[5], 1), 0, POOL - 1).astype(jnp.int32),
        "step_index": jax.random.randint(seeds[6], (1,), 0, 1000).astype(jnp.int32),
    }


quintic_a = 3.4445
quintic_b = -4.775
quintic_c = 2.0315

def orthogonalize(block):
    norm = jnp.sqrt(jnp.sum(block * block)) + 1e-07
    iterate = (block / norm).astype(jnp.bfloat16)
    for turn in range(NS_ITERS):
        gram = jnp.dot(iterate.T, iterate, preferred_element_type=jnp.float32).astype(jnp.bfloat16)
        square = jnp.dot(gram, gram, preferred_element_type=jnp.float32)
        poly = (quintic_b * gram.astype(jnp.float32) + quintic_c * square).astype(jnp.bfloat16)
        iterate = (quintic_a * iterate.astype(jnp.float32) + jnp.dot(iterate, poly, preferred_element_type=jnp.float32)).astype(jnp.bfloat16)
    return iterate

def block_view(matrix):
    shaped = matrix.reshape(GRID, QOUT // GRID, GRID, D // GRID).transpose(0, 2, 1, 3)
    return shaped.reshape(GRID * GRID, QOUT // GRID, D // GRID)

def matrix_view(blocks):
    shaped = blocks.reshape(GRID, GRID, QOUT // GRID, D // GRID).transpose(0, 2, 1, 3)
    return shaped.reshape(QOUT, D)

def gradient(pool_rows, out_grad, chosen_ids):
    chosen = jnp.take(pool_rows, chosen_ids.astype(jnp.int32), axis=0)
    return jnp.dot(out_grad.T, chosen, preferred_element_type=jnp.float32)

def reference(weights, tracker, grad_prev, pool, out_grads, row_ids, step_index):
    levels = REPS.bit_length() - 1
    replica = jnp.arange(REPS, dtype=jnp.int32)
    scale = 0.2 * math.sqrt(QOUT // GRID)
    for step in range(STEPS):
        bit = ((step_index[0] + step) % levels).astype(jnp.int32)
        partner = jnp.bitwise_xor(replica, jnp.left_shift(jnp.ones((), jnp.int32), bit))

        def one(index):
            other = partner[index]
            fresh = gradient(pool[index], out_grads[index, step], row_ids[index, step])
            if step == 0:
                older = grad_prev[index].astype(jnp.float32)
            else:
                older = gradient(pool[index], out_grads[index, step - 1], row_ids[index, step - 1])
            mixed = (0.5 * (tracker[index].astype(jnp.float32) + tracker[other].astype(jnp.float32)) + fresh - older).astype(jnp.bfloat16)
            update = matrix_view(lax.map(orthogonalize, block_view(mixed.astype(jnp.float32))))
            moved = 0.5 * (weights[index].astype(jnp.float32) + weights[other].astype(jnp.float32)) - scale * update.astype(jnp.float32)
            return (moved.astype(jnp.bfloat16), mixed)
        weights, tracker = lax.map(one, replica)
    return (weights, tracker)
```

```python
import functools
import math

import jax
import jax.numpy as jnp
from jax import lax
from jax.experimental import pallas as pl
from jax.experimental.pallas import tpu as pltpu
from jax.sharding import PartitionSpec as P


D = 2048
QOUT = 4096
GRID = 4
NS_ITERS = 2
STEPS = 2
SPLIT = 2
NEAR_SHARES = (2, 5, 5, 4)
FAR_SHARES = (5, 5, 4, 2)
TILE = 256

quintic_a = 3.4445
quintic_b = -4.775
quintic_c = 2.0315


f32 = jnp.float32
bf16 = jnp.bfloat16
dot = functools.partial(jnp.dot, preferred_element_type=f32)


def xor_route(count, mask):
    return [(low, low ^ mask) for low in range(count) if low ^ mask < count]


def send(x, axis, route):
    return lax.ppermute(x, axis, route)


def gather_pieces(x, axis):
    count = lax.axis_size(axis)
    here = lax.axis_index(axis)
    if count & (count - 1):
        whole = lax.all_gather(x, axis, axis=0)
        return [whole[k] for k in range(count)], [jnp.int32(k) for k in range(count)]
    pieces = {0: x}
    mask = count >> 1
    while mask:
        for k, piece in list(pieces.items()):
            pieces[k ^ mask] = send(piece, axis, xor_route(count, mask))
        mask >>= 1
    return [pieces[k] for k in range(count)], [here ^ k for k in range(count)]


def tt(x, y):
    return lax.dot_general(x, y, (((0,), (0,)), ((), ())), preferred_element_type=f32)


def newton_schulz(x_ref, block):
    norm = jnp.sqrt(jnp.sum(block * block)) + 1e-07
    x_ref[...] = (block / norm).astype(bf16)
    lax.fori_loop(0, NS_ITERS, lambda turn, _: newton_schulz_turn(x_ref), None)


def newton_schulz_turn(x_ref):
    x = x_ref[...]
    gram = tt(x, x).astype(bf16)
    poly = (quintic_b * gram.astype(f32) + quintic_c * dot(gram, gram)).astype(bf16)
    x_ref[...] = (quintic_a * x.astype(f32) + dot(x, poly)).astype(bf16)


def call(kernel, out_shape, mib=16, **kw):
    params = pltpu.CompilerParams(vmem_limit_bytes=mib << 20)
    return pl.pallas_call(kernel, out_shape=out_shape, compiler_params=params, **kw)


def loop(count, step):
    lax.fori_loop(0, count, lambda k, _: step(k), None)


def tile(k, size):
    return pl.ds(pl.multiple_of(k * size, size), size)


def prepare(pool_pieces, pool_bases, grad_pieces, token_ids, step):
    count_p, count_g = len(pool_pieces), len(grad_pieces)
    pool_rows, cols = pool_pieces[0].shape
    tokens, rows = grad_pieces[0].shape
    total = count_g * tokens

    def kernel(base_ref, ids_ref, *refs):
        pools, grads, (chosen_ref, turned_ref) = refs[:count_p], refs[count_p:-2], refs[-2:]
        lane = lax.broadcasted_iota(jnp.int32, (tokens, pool_rows), 1)

        def pick(g):
            here = tile(g, tokens)
            own = ids_ref[here, :]
            acc = jnp.zeros((tokens, cols), f32)
            for k in range(count_p):
                hot = jnp.where(own - base_ref[k] == lane, 1.0, 0.0).astype(bf16)
                acc += dot(hot, pools[k][...])
            chosen_ref[here, :] = acc.astype(bf16)

        loop(count_g, pick)
        for g in range(count_g):
            turned_ref[:, g * tokens : (g + 1) * tokens] = grads[g][...].T

    whole = lambda *shape: pl.BlockSpec(shape, lambda i: (0,) * len(shape))
    return call(
        kernel,
        (jax.ShapeDtypeStruct((total, cols), bf16), jax.ShapeDtypeStruct((rows, total), bf16)),
        grid=(1,),
        in_specs=[pl.BlockSpec(memory_space=pltpu.SMEM), pl.BlockSpec((total, 1), lambda i: (step, 0))]
        + [whole(pool_rows, cols)] * count_p
        + [whole(tokens, rows)] * count_g,
        out_specs=(whole(total, cols), whole(rows, total)),
    )(pool_bases, token_ids, *pool_pieces, *grad_pieces)


def first_mix(own, other, older, turned, chosen, row, col, height, width):
    def kernel(own_ref, other_ref, older_ref, turned_ref, chosen_ref, out_ref):
        def mix(k):
            t = tile(k, TILE)
            fresh = dot(turned_ref[t, :], chosen_ref[...])
            mean = 0.5 * (own_ref[t, :].astype(f32) + other_ref[t, :].astype(f32))
            out_ref[t, :] = (mean + fresh - older_ref[t, :].astype(f32)).astype(bf16)

        loop(height // TILE, mix)

    tokens = chosen.shape[0]
    piece = pl.BlockSpec((height, width), lambda i: (row, col))
    alone = pl.BlockSpec((height, width), lambda i: (0, 0))
    return call(
        kernel,
        jax.ShapeDtypeStruct((height, width), bf16),
        grid=(1,),
        in_specs=[
            piece,
            alone,
            piece,
            pl.BlockSpec((height, tokens), lambda i: (row, 0)),
            pl.BlockSpec((tokens, width), lambda i: (0, col)),
        ],
        out_specs=alone,
    )(own, other, older, turned, chosen)


def stacked(refs):
    return jnp.concatenate([r[...] for r in refs], axis=0)


def newton_schulz(x_ref, count):
    def scale(k):
        block = x_ref[k].astype(f32)
        norm = jnp.sqrt(jnp.sum(block * block)) + 1e-07
        x_ref[k] = (block * (1.0 / norm)).astype(bf16)
        loop(NS_ITERS, lambda _: turn(k))

    def turn(k):
        x = x_ref[k]
        gram = tt(x, x).astype(bf16)
        poly = (quintic_b * gram.astype(f32) + quintic_c * dot(gram, gram)).astype(bf16)
        x_ref[k] = (quintic_a * x.astype(f32) + dot(x, poly)).astype(bf16)

    loop(count, scale)


def orthogonal(blocks):
    pieces = len(blocks[0])
    height, width = blocks[0][0].shape
    height *= pieces

    def kernel(*refs):
        x_ref = refs[-1]
        for k in range(len(blocks)):
            x_ref[k] = stacked(refs[k * pieces : (k + 1) * pieces])
        newton_schulz(x_ref, len(blocks))

    return call(
        kernel, jax.ShapeDtypeStruct((len(blocks), height, width), bf16)
    )(*[piece for block in blocks for piece in block])


def second_mix(mine, theirs, grads, row, col, whole, previous):
    pieces = len(mine)
    height, width = mine[0].shape
    height *= pieces

    def kernel(*refs):
        mine_refs, theirs_refs = refs[:pieces], refs[pieces : 2 * pieces]
        turned_1, chosen_1, turned_0, chosen_0 = refs[2 * pieces : 2 * pieces + 4]
        tracker_ref, update_ref, x_ref, y_ref = refs[-4:]
        x_ref[0] = stacked(theirs_refs)
        y_ref[...] = stacked(mine_refs)

        def mix(k):
            t = tile(k, TILE)
            fresh = dot(turned_1[t, :], chosen_1[...]) - dot(turned_0[t, :], chosen_0[...])
            mean = 0.5 * (y_ref[t, :].astype(f32) + x_ref[0, t, :].astype(f32))
            mixed = (mean + fresh).astype(bf16)
            tracker_ref[t, :] = mixed
            x_ref[1, t, :] = mixed

        loop(height // TILE, mix)
        newton_schulz(x_ref, 2)
        update_ref[...] = 0.5 * x_ref[0].astype(f32) + x_ref[1].astype(f32)

    alone = pl.BlockSpec((height // pieces, width), lambda i: (0, 0))
    operands = [*mine, *theirs, *grads]
    in_specs = [alone] * (2 * pieces)
    for turned, chosen in zip(grads[::2], grads[1::2]):
        in_specs += [pl.BlockSpec((height, turned.shape[1]), lambda i: (row, 0))]
        in_specs += [pl.BlockSpec((chosen.shape[0], width), lambda i: (0, col))]
    aliases = {}
    if previous is not None:
        aliases = {len(operands): 0}
        operands += [previous]
        in_specs += [pl.BlockSpec(memory_space=pl.ANY)]
    return call(
        kernel,
        mib=32,
        out_shape=(jax.ShapeDtypeStruct((1, *whole), bf16), jax.ShapeDtypeStruct((height, width), f32)),
        grid=(1,),
        in_specs=in_specs,
        out_specs=(
            pl.BlockSpec((None, height, width), lambda i: (0, row, col)),
            pl.BlockSpec((height, width), lambda i: (0, 0)),
        ),
        scratch_shapes=[pltpu.VMEM((2, height, width), bf16), pltpu.VMEM((height, width), bf16)],
        input_output_aliases=aliases,
    )(*operands)


def apply(means, first, updates, scale, at, blocks, whole, previous):
    rows, cols = means[0].shape
    _, height, width = first.shape
    unit = math.gcd(at, rows) if at else rows
    steps = rows // unit

    def kernel(*refs):
        mean_refs, (first_ref, *update_refs) = refs[: len(means)], refs[len(means) : len(operands)]
        out_ref = refs[-1]
        for c in range(blocks):
            cut = slice(c * width, (c + 1) * width)
            mean = sum(r[:, cut].astype(f32) for r in mean_refs)
            update = 0.5 * first_ref[c].astype(f32) + update_refs[c][...]
            out_ref[:, cut] = (mean - scale * update).astype(bf16)

    row = at // height
    into = lambda i: (at % height) // unit + i
    operands = [*means, first, *updates[row * blocks : (row + 1) * blocks]]
    in_specs = [pl.BlockSpec((unit, cols), lambda i: (i, 0))] * len(means)
    in_specs += [pl.BlockSpec((blocks, unit, width), lambda i: (row, into(i), 0))]
    in_specs += [pl.BlockSpec((unit, width), lambda i: (into(i), 0))] * blocks
    aliases = {}
    if previous is not None:
        aliases = {len(operands): 0}
    call_operands = operands + ([previous] if previous is not None else [])
    return call(
        kernel,
        jax.ShapeDtypeStruct((1, *whole), bf16),
        grid=(steps,),
        in_specs=in_specs + [pl.BlockSpec(memory_space=pl.ANY)] * len(aliases),
        out_specs=pl.BlockSpec((None, unit, cols), lambda i: (0, at // unit + i, 0)),
        input_output_aliases=aliases,
    )(*call_operands)


def mean_of_four(own, first_route, second_route):
    count = lax.axis_size("rep")

    def both(x, y, factor):
        return (factor * (x.astype(f32) + y.astype(f32))).astype(bf16)

    if count != 4:
        partial = both(own, send(own, "rep", first_route), 1.0)
        across = send(partial, "rep", second_route)
        return [both(partial, across, 0.25)]
    place = lax.axis_index("rep")
    inner = (place == 1) | (place == 2)
    partial = both(own, send(own, "rep", [(0, 1), (3, 2)]), 1.0)
    across = send(partial, "rep", [(1, 2), (2, 1)])
    mean = both(partial, across, jnp.where(inner, 0.25, 0.0))
    return [mean, send(mean, "rep", [(1, 0), (2, 3)])]


def two_steps(first_mask, second_mask, weights, tracker, grad_prev, pool, out_grads, row_ids):
    count = lax.axis_size("rep")
    rows, cols = weights.shape
    height, width = QOUT // GRID, D // GRID
    piece = height // SPLIT
    scale = 0.2 * math.sqrt(QOUT // GRID)
    first_route, second_route = xor_route(count, first_mask), xor_route(count, second_mask)

    tokens = out_grads.shape[1]
    pool_pieces, pool_from = gather_pieces(pool, "row")
    pool_bases = jnp.stack(pool_from).astype(jnp.int32) * pool.shape[0]
    grad_pieces = []
    for step in range(STEPS):
        pieces, grad_from = gather_pieces(out_grads[step], "col")
        grad_pieces.append(pieces)
    ids = [
        lax.dynamic_slice(row_ids, (step, place * tokens), (1, tokens))
        for step in range(STEPS)
        for place in grad_from
    ]
    ids = jnp.concatenate(ids, axis=1).reshape(-1, 1)
    grads = []
    for step in range(STEPS):
        chosen, turned = prepare(pool_pieces, pool_bases, grad_pieces[step], ids, step)
        grads = [turned, chosen, *grads]

    def part(x, r, c):
        return lax.slice(x, (r * piece, c * width), ((r + 1) * piece, (c + 1) * width))

    blocks = [(r, c) for r in range(rows // height) for c in range(cols // width)]
    mine, theirs = [], []
    for row, col in blocks:
        mine.append([])
        theirs.append([])
        for s in range(SPLIT):
            r = row * SPLIT + s
            other = send(part(tracker, r, col), "rep", first_route)
            mixed = first_mix(tracker, other, grad_prev, *grads[2:], r, col, piece, width)
            mine[-1].append(mixed)
            theirs[-1].append(send(mixed, "rep", second_route))
    first = orthogonal(mine)
    new_tracker, updates = None, []
    for b, (row, col) in enumerate(blocks):
        new_tracker, update = second_mix(
            mine[b], theirs[b], grads, row, col, weights.shape, new_tracker
        )
        updates.append(update)

    new_weights, at = None, 0
    shares = NEAR_SHARES if first_mask == 1 else FAR_SHARES
    for share in shares:
        size = rows * share // sum(shares)
        own = lax.optimization_barrier(lax.slice_in_dim(weights, at, at + size))
        means = mean_of_four(own, first_route, second_route)
        new_weights = apply(
            means, first, updates, scale, at, cols // width, weights.shape, new_weights
        )
        at += size
    return new_weights, new_tracker


def body(weights, tracker, grad_prev, pool, out_grads, row_ids, step_index):
    levels = lax.axis_size("rep").bit_length() - 1

    def branch(level, *args):
        return two_steps(1 << level, 1 << (level + 1) % levels, *args)

    return lax.switch(
        step_index[0] % levels,
        [functools.partial(branch, level) for level in range(levels)],
        weights[0],
        tracker[0],
        grad_prev[0],
        pool[0],
        out_grads[0],
        row_ids[0],
    )


def solution(mesh):
    in_specs = (
        P("rep", "row", "col"),
        P("rep", "row", "col"),
        P("rep", "row", "col"),
        P("rep", "row", "col"),
        P("rep", None, "col", "row"),
        P("rep", None, None),
        P(),
    )
    out_specs = (P("rep", "row", "col"), P("rep", "row", "col"))
    return jax.shard_map(body, mesh=mesh, in_specs=in_specs, out_specs=out_specs, check_vma=False)
```

```python
import functools
import math

import jax
import jax.numpy as jnp
from jax import lax
from jax.experimental import pallas as pl
from jax.experimental.pallas import tpu as pltpu
from jax.sharding import PartitionSpec as P


D = 2048
QOUT = 4096
GRID = 4
NS_ITERS = 2
STEPS = 2
SPLIT = 2
NEAR_PLAN = ((4, 4, 4, 4), 3, False)
FAR_PLAN = ((4, 4, 4, 4), 2, True)
TILE = 256

quintic_a = 3.4445
quintic_b = -4.775
quintic_c = 2.0315


f32 = jnp.float32
bf16 = jnp.bfloat16
dot = functools.partial(jnp.dot, preferred_element_type=f32)


def xor_route(count, mask):
    return [(low, low ^ mask) for low in range(count) if low ^ mask < count]


def send(x, axis, route):
    return lax.ppermute(x, axis, route)


def swap(x, mask, relay):
    count = lax.axis_size("rep")
    if not relay or count != 4 or mask != 2:
        return [send(x, "rep", xor_route(count, mask))]
    inward = send(x, "rep", [(0, 1), (3, 2)])
    to_inner = send(inward, "rep", [(1, 2), (2, 1)])
    across = send(x, "rep", [(1, 2), (2, 1)])
    return [to_inner, send(across, "rep", [(1, 0), (2, 3)])]


def gather_pieces(x, axis):
    count = lax.axis_size(axis)
    here = lax.axis_index(axis)
    if count & (count - 1):
        whole = lax.all_gather(x, axis, axis=0)
        return [whole[k] for k in range(count)], [jnp.int32(k) for k in range(count)]
    pieces = {0: x}
    mask = count >> 1
    while mask:
        for k, piece in list(pieces.items()):
            pieces[k ^ mask] = send(piece, axis, xor_route(count, mask))
        mask >>= 1
    return [pieces[k] for k in range(count)], [here ^ k for k in range(count)]


def tt(x, y):
    return lax.dot_general(x, y, (((0,), (0,)), ((), ())), preferred_element_type=f32)


def newton_schulz(x_ref, block):
    norm = jnp.sqrt(jnp.sum(block * block)) + 1e-07
    x_ref[...] = (block / norm).astype(bf16)
    lax.fori_loop(0, NS_ITERS, lambda turn, _: newton_schulz_turn(x_ref), None)


def newton_schulz_turn(x_ref):
    x = x_ref[...]
    gram = tt(x, x).astype(bf16)
    poly = (quintic_b * gram.astype(f32) + quintic_c * dot(gram, gram)).astype(bf16)
    x_ref[...] = (quintic_a * x.astype(f32) + dot(x, poly)).astype(bf16)


def in_hbm(x):
    return pltpu.with_memory_space_constraint(x, pltpu.HBM)


def single(shape, index):
    return pl.BlockSpec(shape, index, pipeline_mode=pl.Buffered(1))


def call(kernel, out_shape, mib=12, **kw):
    params = pltpu.CompilerParams(vmem_limit_bytes=mib << 20)
    return pl.pallas_call(kernel, out_shape=out_shape, compiler_params=params, **kw)


def loop(count, step):
    lax.fori_loop(0, count, lambda k, _: step(k), None)


def tile(k, size):
    return pl.ds(pl.multiple_of(k * size, size), size)


def prepare(pool_pieces, pool_bases, grad_pieces, token_ids, step):
    count_p, count_g = len(pool_pieces), len(grad_pieces)
    pool_rows, cols = pool_pieces[0].shape
    tokens, rows = grad_pieces[0].shape
    total = count_g * tokens

    def kernel(base_ref, ids_ref, *refs):
        pools, grads, (chosen_ref, turned_ref) = refs[:count_p], refs[count_p:-2], refs[-2:]
        lane = lax.broadcasted_iota(jnp.int32, (tokens, pool_rows), 1)

        def pick(g):
            here = tile(g, tokens)
            own = ids_ref[here, :]
            acc = jnp.zeros((tokens, cols), f32)
            for k in range(count_p):
                hot = jnp.where(own - base_ref[k] == lane, 1.0, 0.0).astype(bf16)
                acc += dot(hot, pools[k][...])
            chosen_ref[here, :] = acc.astype(bf16)

        loop(count_g, pick)
        for g in range(count_g):
            turned_ref[:, g * tokens : (g + 1) * tokens] = grads[g][...].T

    whole = lambda *shape: single(shape, lambda i: (0,) * len(shape))
    return call(
        kernel,
        (jax.ShapeDtypeStruct((total, cols), bf16), jax.ShapeDtypeStruct((rows, total), bf16)),
        grid=(1,),
        in_specs=[pl.BlockSpec(memory_space=pltpu.SMEM), pl.BlockSpec((total, 1), lambda i: (step, 0))]
        + [whole(pool_rows, cols)] * count_p
        + [whole(tokens, rows)] * count_g,
        out_specs=(whole(total, cols), whole(rows, total)),
    )(pool_bases, token_ids, *pool_pieces, *grad_pieces)


def first_mix(own, others, older, turned, chosen, row, col, height, width):
    def kernel(own_ref, older_ref, turned_ref, chosen_ref, *refs):
        *other_refs, out_ref = refs

        def mix(k):
            t = tile(k, TILE)
            fresh = dot(turned_ref[t, :], chosen_ref[...])
            mean = 0.5 * (own_ref[t, :].astype(f32) + sum(r[t, :].astype(f32) for r in other_refs))
            out_ref[t, :] = (mean + fresh - older_ref[t, :].astype(f32)).astype(bf16)

        loop(height // TILE, mix)

    tokens = chosen.shape[0]
    piece = single((height, width), lambda i: (row, col))
    alone = single((height, width), lambda i: (0, 0))
    return call(
        kernel,
        jax.ShapeDtypeStruct((height, width), bf16),
        grid=(1,),
        in_specs=[
            piece,
            piece,
            single((height, tokens), lambda i: (row, 0)),
            single((tokens, width), lambda i: (0, col)),
        ]
        + [alone] * len(others),
        out_specs=alone,
    )(in_hbm(own), in_hbm(older), turned, chosen, *others)


def stacked(refs):
    return jnp.concatenate([r[...] for r in refs], axis=0)


def newton_schulz(x_ref, count):
    def scale(k):
        block = x_ref[k].astype(f32)
        norm = jnp.sqrt(jnp.sum(block * block)) + 1e-07
        x_ref[k] = (block * (1.0 / norm)).astype(bf16)
        loop(NS_ITERS, lambda _: turn(k))

    def turn(k):
        x = x_ref[k]
        gram = tt(x, x).astype(bf16)
        poly = (quintic_b * gram.astype(f32) + quintic_c * dot(gram, gram)).astype(bf16)
        x_ref[k] = (quintic_a * x.astype(f32) + dot(x, poly)).astype(bf16)

    loop(count, scale)


def orthogonal(pieces):
    height, width = pieces[0].shape
    height *= len(pieces)

    def kernel(*refs):
        refs[-1][0] = stacked(refs[:-1])
        newton_schulz(refs[-1], 1)

    return call(kernel, jax.ShapeDtypeStruct((1, height, width), bf16))(*pieces)


def sliver(*sizes):
    return math.gcd(64, *sizes)


def second_mix(mine, theirs, grads, first, means, scale, block, whole, previous):
    pieces = len(mine)
    height, width = mine[0].shape
    height *= pieces
    sizes = [parts[0].shape[0] for parts in means]
    early = sum(sizes)
    flat = [part for parts in means for part in parts]
    each = len(flat) // len(means)
    received, parts = [part for pieces_of in theirs for part in pieces_of], len(theirs[0])
    cut = slice(block * width, (block + 1) * width)
    outs = 3 if early < height else 2

    def kernel(*refs):
        mine_refs, refs = refs[:pieces], refs[pieces:]
        theirs_refs, refs = refs[: len(received)], refs[len(received) :]
        turned_1, chosen_1, turned_0, chosen_0, first_ref = refs[:5]
        mean_refs = refs[5 : 5 + len(flat)]
        *out_refs, x_ref, y_ref, tracker_ref, weights_ref, sems = refs[-outs - 5 :]
        x_ref[0] = sum(stacked(theirs_refs[part::parts]) for part in range(parts))
        y_ref[...] = stacked(mine_refs)

        def mix(k):
            t = tile(k, TILE)
            fresh = dot(turned_1[t, :], chosen_1[:, cut]) - dot(turned_0[t, :], chosen_0[:, cut])
            mean = 0.5 * (y_ref[t, :].astype(f32) + x_ref[0, t, :].astype(f32))
            mixed = (mean + fresh).astype(bf16)
            tracker_ref[t, :] = mixed
            x_ref[1, t, :] = mixed

        def update(t):
            both = first_ref[0, t, :].astype(f32) + x_ref[0, t, :].astype(f32)
            return 0.5 * both + x_ref[1, t, :].astype(f32)

        loop(height // TILE, mix)
        tracker_copy = pltpu.make_async_copy(tracker_ref, out_refs[0].at[0, :, cut], sems.at[0])
        tracker_copy.start()
        newton_schulz(x_ref, 2)
        at = 0
        for p, size in enumerate(sizes):
            unit = sliver(size, at)

            def weigh(k, at=at, unit=unit, parts=mean_refs[p * each : (p + 1) * each]):
                mean = sum(r[tile(k, unit), cut].astype(f32) for r in parts)
                t = pl.ds(pl.multiple_of(at + k * unit, unit), unit)
                weights_ref[t, :] = (mean - scale * update(t)).astype(bf16)

            loop(size // unit, weigh)
            at += size
        weights_copy = pltpu.make_async_copy(weights_ref, out_refs[1].at[0, :early, cut], sems.at[1])
        weights_copy.start()
        if outs == 3:
            unit = sliver(height - early, early)

            def keep(k):
                t = pl.ds(pl.multiple_of(early + k * unit, unit), unit)
                out_refs[2][tile(k, unit), :] = update(t)

            loop((height - early) // unit, keep)
        tracker_copy.wait()
        weights_copy.wait()

    vmem = pl.BlockSpec(memory_space=pltpu.VMEM)
    apart = pl.BlockSpec(memory_space=pltpu.HBM)
    operands = [*mine, *received, *grads, first, *flat]
    in_specs = [vmem] * len(operands)
    aliases = {}
    if previous is not None:
        aliases = {len(operands): 0, len(operands) + 1: 1}
        operands += list(previous)
        in_specs += [apart] * 2
    out_shape = [jax.ShapeDtypeStruct((1, *whole), bf16)] * 2
    if outs == 3:
        out_shape += [jax.ShapeDtypeStruct((height - early, width), f32)]
    return call(
        kernel,
        mib=24,
        out_shape=out_shape,
        in_specs=in_specs,
        out_specs=[apart] * 2 + [vmem] * (outs - 2),
        scratch_shapes=[
            pltpu.VMEM((2, height, width), bf16),
            pltpu.VMEM((height, width), bf16),
            pltpu.VMEM((height, width), bf16),
            pltpu.VMEM((early, width), bf16),
            pltpu.SemaphoreType.DMA((2,)),
        ],
        input_output_aliases=aliases,
    )(*operands)


def apply(means, updates, scale, at, start, whole, previous):
    rows, cols = means[0].shape
    unit = math.gcd(rows, at, at - start) if at > start else math.gcd(rows, at)
    width = updates[0].shape[1]

    def kernel(*refs):
        mean_refs, update_refs = refs[: len(means)], refs[len(means) : len(means) + len(updates)]
        out_ref = refs[-1]
        for c, update_ref in enumerate(update_refs):
            cut = slice(c * width, (c + 1) * width)
            mean = sum(r[:, cut].astype(f32) for r in mean_refs)
            out_ref[:, cut] = (mean - scale * update_ref[...]).astype(bf16)

    operands = [*means, *updates, previous]
    return call(
        kernel,
        jax.ShapeDtypeStruct((1, *whole), bf16),
        grid=(rows // unit,),
        in_specs=[pl.BlockSpec((unit, cols), lambda i: (i, 0))] * len(means)
        + [pl.BlockSpec((unit, width), lambda i: ((at - start) // unit + i, 0))] * len(updates)
        + [pl.BlockSpec(memory_space=pl.ANY)],
        out_specs=pl.BlockSpec((None, unit, cols), lambda i: (0, at // unit + i, 0)),
        input_output_aliases={len(operands) - 1: 0},
    )(*operands)


def mean_of_four(own, first_route, second_route):
    count = lax.axis_size("rep")

    def both(x, y, factor):
        return (factor * (x.astype(f32) + y.astype(f32))).astype(bf16)

    if count != 4:
        partial = both(own, send(own, "rep", first_route), 1.0)
        across = send(partial, "rep", second_route)
        return [both(partial, across, 0.25)]
    place = lax.axis_index("rep")
    inner = (place == 1) | (place == 2)
    partial = both(own, send(own, "rep", [(0, 1), (3, 2)]), 1.0)
    across = send(partial, "rep", [(1, 2), (2, 1)])
    mean = both(partial, across, jnp.where(inner, 0.25, 0.0))
    return [mean, send(mean, "rep", [(1, 0), (2, 3)])]


def two_steps(first_mask, second_mask, weights, tracker, grad_prev, pool, out_grads, row_ids):
    count = lax.axis_size("rep")
    rows, cols = weights.shape
    height, width = QOUT // GRID, D // GRID
    assert rows == height and cols % width == 0
    piece = height // SPLIT
    scale = 0.2 * math.sqrt(QOUT // GRID)
    first_route, second_route = xor_route(count, first_mask), xor_route(count, second_mask)

    tokens = out_grads.shape[1]
    pool_pieces, pool_from = gather_pieces(pool, "row")
    pool_bases = jnp.stack(pool_from).astype(jnp.int32) * pool.shape[0]
    grad_pieces = []
    for step in range(STEPS):
        pieces, grad_from = gather_pieces(out_grads[step], "col")
        grad_pieces.append(pieces)
    ids = [
        lax.dynamic_slice(row_ids, (step, place * tokens), (1, tokens))
        for step in range(STEPS)
        for place in grad_from
    ]
    ids = jnp.concatenate(ids, axis=1).reshape(-1, 1)
    grads = []
    for step in range(STEPS):
        chosen, turned = prepare(pool_pieces, pool_bases, grad_pieces[step], ids, step)
        grads = [turned, chosen, *grads]

    def part(x, r, c):
        return lax.slice(x, (r * piece, c * width), ((r + 1) * piece, (c + 1) * width))

    shares, early, relay = NEAR_PLAN if first_mask == 1 else FAR_PLAN
    mine, theirs = [], []
    for col in range(cols // width):
        mine.append([])
        theirs.append([])
        for r in range(SPLIT):
            k = col * SPLIT + r
            others = swap(part(tracker, r, col), first_mask, relay)
            mixed = first_mix(tracker, others, grad_prev, *grads[2:], r, col, piece, width)
            mine[-1].append(mixed)
            theirs[-1].append(swap(mixed, second_mask, relay))
    first = [orthogonal(mine[col]) for col in range(len(mine))]

    ends = [rows * sum(shares[: k + 1]) // sum(shares) for k in range(len(shares))]
    cuts = list(zip([0, *ends], ends))
    means = []
    for k, (low, high) in enumerate(cuts):
        own = lax.optimization_barrier(lax.slice_in_dim(weights, low, high))
        means.append(mean_of_four(own, first_route, second_route))

    results, updates = None, []
    for col in range(cols // width):
        *results, update = *second_mix(
            mine[col], theirs[col], grads, first[col], means[:early], scale, col,
            weights.shape, results,
        ), None
        if early < len(shares):
            *results, update = results
        updates.append(update)
    new_tracker, new_weights = results
    for k in range(early, len(shares)):
        new_weights = apply(means[k], updates, scale, cuts[k][0], cuts[early][0], weights.shape, new_weights)
    return new_weights, new_tracker


def body(weights, tracker, grad_prev, pool, out_grads, row_ids, step_index):
    levels = lax.axis_size("rep").bit_length() - 1

    def branch(level, *args):
        return two_steps(1 << level, 1 << (level + 1) % levels, *args)

    return lax.switch(
        step_index[0] % levels,
        [functools.partial(branch, level) for level in range(levels)],
        weights[0],
        tracker[0],
        grad_prev[0],
        pool[0],
        out_grads[0],
        row_ids[0],
    )


def solution(mesh):
    in_specs = (
        P("rep", "row", "col"),
        P("rep", "row", "col"),
        P("rep", "row", "col"),
        P("rep", "row", "col"),
        P("rep", None, "col", "row"),
        P("rep", None, None),
        P(),
    )
    out_specs = (P("rep", "row", "col"), P("rep", "row", "col"))
    return jax.shard_map(body, mesh=mesh, in_specs=in_specs, out_specs=out_specs, check_vma=False)
```

```python
import functools
import math

import jax
import jax.numpy as jnp
from jax import lax
from jax.experimental import pallas as pl
from jax.experimental.pallas import tpu as pltpu
from jax.sharding import PartitionSpec as P


D = 2048
QOUT = 4096
GRID = 4
NS_ITERS = 2
STEPS = 2
SPLIT = 2
NEAR_PLAN = ((4, 4, 4, 4), 4, False)
FAR_PLAN = ((4, 4, 4, 4), 2, True)
TILE = 256

quintic_a = 3.4445
quintic_b = -4.775
quintic_c = 2.0315


f32 = jnp.float32
bf16 = jnp.bfloat16
dot = functools.partial(jnp.dot, preferred_element_type=f32)


def xor_route(count, mask):
    return [(low, low ^ mask) for low in range(count) if low ^ mask < count]


def send(x, axis, route):
    return lax.ppermute(x, axis, route)


def swap(x, mask, relay):
    count = lax.axis_size("rep")
    if not relay or count != 4 or mask != 2:
        return [send(x, "rep", xor_route(count, mask))]
    inward = send(x, "rep", [(0, 1), (3, 2)])
    to_inner = send(inward, "rep", [(1, 2), (2, 1)])
    across = send(x, "rep", [(1, 2), (2, 1)])
    return [to_inner, send(across, "rep", [(1, 0), (2, 3)])]


def gather_pieces(x, axis):
    count = lax.axis_size(axis)
    here = lax.axis_index(axis)
    if count & (count - 1):
        whole = lax.all_gather(x, axis, axis=0)
        return [whole[k] for k in range(count)], [jnp.int32(k) for k in range(count)]
    pieces = {0: x}
    mask = count >> 1
    while mask:
        for k, piece in list(pieces.items()):
            pieces[k ^ mask] = send(piece, axis, xor_route(count, mask))
        mask >>= 1
    return [pieces[k] for k in range(count)], [here ^ k for k in range(count)]


def tt(x, y):
    return lax.dot_general(x, y, (((0,), (0,)), ((), ())), preferred_element_type=f32)


def newton_schulz(x_ref, block):
    norm = jnp.sqrt(jnp.sum(block * block)) + 1e-07
    x_ref[...] = (block / norm).astype(bf16)
    lax.fori_loop(0, NS_ITERS, lambda turn, _: newton_schulz_turn(x_ref), None)


def newton_schulz_turn(x_ref):
    x = x_ref[...]
    gram = tt(x, x).astype(bf16)
    poly = (quintic_b * gram.astype(f32) + quintic_c * dot(gram, gram)).astype(bf16)
    x_ref[...] = (quintic_a * x.astype(f32) + dot(x, poly)).astype(bf16)


def in_hbm(x):
    return pltpu.with_memory_space_constraint(x, pltpu.HBM)


def single(shape, index):
    return pl.BlockSpec(shape, index, pipeline_mode=pl.Buffered(1))


def call(kernel, out_shape, mib=12, **kw):
    params = pltpu.CompilerParams(vmem_limit_bytes=mib << 20)
    return pl.pallas_call(kernel, out_shape=out_shape, compiler_params=params, **kw)


def loop(count, step):
    lax.fori_loop(0, count, lambda k, _: step(k), None)


def tile(k, size):
    return pl.ds(pl.multiple_of(k * size, size), size)


def prepare(pool_pieces, pool_bases, grad_pieces, token_ids, step):
    count_p, count_g = len(pool_pieces), len(grad_pieces)
    pool_rows, cols = pool_pieces[0].shape
    tokens, rows = grad_pieces[0].shape
    total = count_g * tokens

    def kernel(base_ref, ids_ref, *refs):
        pools, grads, (chosen_ref, turned_ref) = refs[:count_p], refs[count_p:-2], refs[-2:]
        lane = lax.broadcasted_iota(jnp.int32, (tokens, pool_rows), 1)

        def pick(g):
            here = tile(g, tokens)
            own = ids_ref[here, :]
            acc = jnp.zeros((tokens, cols), f32)
            for k in range(count_p):
                hot = jnp.where(own - base_ref[k] == lane, 1.0, 0.0).astype(bf16)
                acc += dot(hot, pools[k][...])
            chosen_ref[here, :] = acc.astype(bf16)

        loop(count_g, pick)
        for g in range(count_g):
            turned_ref[:, g * tokens : (g + 1) * tokens] = grads[g][...].T

    whole = lambda *shape: single(shape, lambda i: (0,) * len(shape))
    return call(
        kernel,
        (jax.ShapeDtypeStruct((total, cols), bf16), jax.ShapeDtypeStruct((rows, total), bf16)),
        grid=(1,),
        in_specs=[pl.BlockSpec(memory_space=pltpu.SMEM), pl.BlockSpec((total, 1), lambda i: (step, 0))]
        + [whole(pool_rows, cols)] * count_p
        + [whole(tokens, rows)] * count_g,
        out_specs=(whole(total, cols), whole(rows, total)),
    )(pool_bases, token_ids, *pool_pieces, *grad_pieces)


def first_mix(own, others, older, turned, chosen, row, col, height, width):
    def kernel(own_ref, older_ref, turned_ref, chosen_ref, *refs):
        *other_refs, out_ref = refs

        def mix(k):
            t = tile(k, TILE)
            fresh = dot(turned_ref[t, :], chosen_ref[...])
            mean = 0.5 * (own_ref[t, :].astype(f32) + sum(r[t, :].astype(f32) for r in other_refs))
            out_ref[t, :] = (mean + fresh - older_ref[t, :].astype(f32)).astype(bf16)

        loop(height // TILE, mix)

    tokens = chosen.shape[0]
    piece = single((height, width), lambda i: (row, col))
    alone = single((height, width), lambda i: (0, 0))
    return call(
        kernel,
        jax.ShapeDtypeStruct((height, width), bf16),
        grid=(1,),
        in_specs=[
            piece,
            piece,
            single((height, tokens), lambda i: (row, 0)),
            single((tokens, width), lambda i: (0, col)),
        ]
        + [alone] * len(others),
        out_specs=alone,
    )(in_hbm(own), in_hbm(older), turned, chosen, *others)


def stacked(refs):
    return jnp.concatenate([r[...] for r in refs], axis=0)


def newton_schulz(x_ref, count):
    def scale(k):
        block = x_ref[k].astype(f32)
        norm = jnp.sqrt(jnp.sum(block * block)) + 1e-07
        x_ref[k] = (block * (1.0 / norm)).astype(bf16)
        loop(NS_ITERS, lambda _: turn(k))

    def turn(k):
        x = x_ref[k]
        gram = tt(x, x).astype(bf16)
        poly = (quintic_b * gram.astype(f32) + quintic_c * dot(gram, gram)).astype(bf16)
        x_ref[k] = (quintic_a * x.astype(f32) + dot(x, poly)).astype(bf16)

    loop(count, scale)


def orthogonal(pieces, grads, block):
    height, width = pieces[0].shape
    height *= len(pieces)
    cut = slice(block * width, (block + 1) * width)

    def kernel(*refs):
        turned_1, chosen_1, turned_0, chosen_0, x_ref, base_ref = refs[len(pieces) :]
        x_ref[0] = stacked(refs[: len(pieces)])

        def mix(k):
            t = tile(k, TILE)
            fresh = dot(turned_1[t, :], chosen_1[:, cut]) - dot(turned_0[t, :], chosen_0[:, cut])
            base_ref[t, :] = 0.5 * x_ref[0, t, :].astype(f32) + fresh

        loop(height // TILE, mix)
        newton_schulz(x_ref, 1)

    out_shape = (
        jax.ShapeDtypeStruct((1, height, width), bf16),
        jax.ShapeDtypeStruct((height, width), f32),
    )
    return call(kernel, out_shape, mib=16)(*pieces, *grads)


def sliver(*sizes):
    return math.gcd(64, *sizes)


def second_mix(theirs, base, first, means, scale, block, whole, previous):
    height, width = base.shape
    sizes = [parts[0].shape[0] for parts in means]
    early = sum(sizes)
    flat = [part for parts in means for part in parts]
    each = len(flat) // len(means)
    received, parts = [part for pieces_of in theirs for part in pieces_of], len(theirs[0])
    cut = slice(block * width, (block + 1) * width)
    outs = 3 if early < height else 2

    def kernel(*refs):
        *out_refs, x_ref, tracker_ref, weights_ref, sems = refs[-outs - 4 :]
        theirs_refs, refs = refs[: len(received)], refs[len(received) :]
        base_ref, first_ref = refs[:2]
        mean_refs = refs[2 : 2 + len(flat)]
        x_ref[0] = sum(stacked(theirs_refs[part::parts]) for part in range(parts))

        def mix(k):
            t = tile(k, TILE)
            mixed = (base_ref[t, :] + 0.5 * x_ref[0, t, :].astype(f32)).astype(bf16)
            tracker_ref[t, :] = mixed
            x_ref[1, t, :] = mixed

        def update(t):
            both = first_ref[0, t, :].astype(f32) + x_ref[0, t, :].astype(f32)
            return 0.5 * both + x_ref[1, t, :].astype(f32)

        loop(height // TILE, mix)
        tracker_copy = pltpu.make_async_copy(tracker_ref, out_refs[0].at[0, :, cut], sems.at[0])
        tracker_copy.start()
        newton_schulz(x_ref, 2)
        at = 0
        for p, size in enumerate(sizes):
            unit = sliver(size, at)

            def weigh(k, at=at, unit=unit, parts=mean_refs[p * each : (p + 1) * each]):
                mean = sum(r[tile(k, unit), cut].astype(f32) for r in parts)
                t = pl.ds(pl.multiple_of(at + k * unit, unit), unit)
                weights_ref[t, :] = (mean - scale * update(t)).astype(bf16)

            loop(size // unit, weigh)
            at += size
        weights_copy = pltpu.make_async_copy(weights_ref, out_refs[1].at[0, :early, cut], sems.at[1])
        weights_copy.start()
        if outs == 3:
            unit = sliver(height - early, early)

            def keep(k):
                t = pl.ds(pl.multiple_of(early + k * unit, unit), unit)
                out_refs[2][tile(k, unit), :] = update(t)

            loop((height - early) // unit, keep)
        tracker_copy.wait()
        weights_copy.wait()

    vmem = pl.BlockSpec(memory_space=pltpu.VMEM)
    apart = pl.BlockSpec(memory_space=pltpu.HBM)
    operands = [*received, base, first, *flat]
    in_specs = [vmem] * len(operands)
    aliases = {}
    if previous is not None:
        aliases = {len(operands): 0, len(operands) + 1: 1}
        operands += list(previous)
        in_specs += [apart] * 2
    out_shape = [jax.ShapeDtypeStruct((1, *whole), bf16)] * 2
    if outs == 3:
        out_shape += [jax.ShapeDtypeStruct((height - early, width), f32)]
    return call(
        kernel,
        mib=24,
        out_shape=out_shape,
        in_specs=in_specs,
        out_specs=[apart] * 2 + [vmem] * (outs - 2),
        scratch_shapes=[
            pltpu.VMEM((2, height, width), bf16),
            pltpu.VMEM((height, width), bf16),
            pltpu.VMEM((early, width), bf16),
            pltpu.SemaphoreType.DMA((2,)),
        ],
        input_output_aliases=aliases,
    )(*operands)


def apply(means, updates, scale, at, start, whole, previous):
    rows, cols = means[0].shape
    unit = math.gcd(rows, at, at - start) if at > start else math.gcd(rows, at)
    width = updates[0].shape[1]

    def kernel(*refs):
        mean_refs, update_refs = refs[: len(means)], refs[len(means) : len(means) + len(updates)]
        out_ref = refs[-1]
        for c, update_ref in enumerate(update_refs):
            cut = slice(c * width, (c + 1) * width)
            mean = sum(r[:, cut].astype(f32) for r in mean_refs)
            out_ref[:, cut] = (mean - scale * update_ref[...]).astype(bf16)

    operands = [*means, *updates, previous]
    return call(
        kernel,
        jax.ShapeDtypeStruct((1, *whole), bf16),
        grid=(rows // unit,),
        in_specs=[pl.BlockSpec((unit, cols), lambda i: (i, 0))] * len(means)
        + [pl.BlockSpec((unit, width), lambda i: ((at - start) // unit + i, 0))] * len(updates)
        + [pl.BlockSpec(memory_space=pl.ANY)],
        out_specs=pl.BlockSpec((None, unit, cols), lambda i: (0, at // unit + i, 0)),
        input_output_aliases={len(operands) - 1: 0},
    )(*operands)


def mean_of_four(own, first_route, second_route):
    count = lax.axis_size("rep")

    def both(x, y, factor):
        return (factor * (x.astype(f32) + y.astype(f32))).astype(bf16)

    if count != 4:
        partial = both(own, send(own, "rep", first_route), 1.0)
        across = send(partial, "rep", second_route)
        return [both(partial, across, 0.25)]
    place = lax.axis_index("rep")
    inner = (place == 1) | (place == 2)
    partial = both(own, send(own, "rep", [(0, 1), (3, 2)]), 1.0)
    across = send(partial, "rep", [(1, 2), (2, 1)])
    mean = both(partial, across, jnp.where(inner, 0.25, 0.0))
    return [mean, send(mean, "rep", [(1, 0), (2, 3)])]


def two_steps(first_mask, second_mask, weights, tracker, grad_prev, pool, out_grads, row_ids):
    count = lax.axis_size("rep")
    rows, cols = weights.shape
    height, width = QOUT // GRID, D // GRID
    assert rows == height and cols % width == 0
    piece = height // SPLIT
    scale = 0.2 * math.sqrt(QOUT // GRID)
    first_route, second_route = xor_route(count, first_mask), xor_route(count, second_mask)

    tokens = out_grads.shape[1]
    pool_pieces, pool_from = gather_pieces(pool, "row")
    pool_bases = jnp.stack(pool_from).astype(jnp.int32) * pool.shape[0]
    grad_pieces = []
    for step in range(STEPS):
        pieces, grad_from = gather_pieces(out_grads[step], "col")
        grad_pieces.append(pieces)
    ids = [
        lax.dynamic_slice(row_ids, (step, place * tokens), (1, tokens))
        for step in range(STEPS)
        for place in grad_from
    ]
    ids = jnp.concatenate(ids, axis=1).reshape(-1, 1)
    grads = []
    for step in range(STEPS):
        chosen, turned = prepare(pool_pieces, pool_bases, grad_pieces[step], ids, step)
        grads = [turned, chosen, *grads]

    def part(x, r, c):
        return lax.slice(x, (r * piece, c * width), ((r + 1) * piece, (c + 1) * width))

    shares, early, relay = NEAR_PLAN if first_mask == 1 else FAR_PLAN
    mine, theirs = [], []
    for col in range(cols // width):
        mine.append([])
        theirs.append([])
        for r in range(SPLIT):
            k = col * SPLIT + r
            others = swap(part(tracker, r, col), first_mask, relay)
            mixed = first_mix(tracker, others, grad_prev, *grads[2:], r, col, piece, width)
            mine[-1].append(mixed)
            theirs[-1].append(swap(mixed, second_mask, relay))
    own = [orthogonal(mine[col], grads, col) for col in range(len(mine))]

    ends = [rows * sum(shares[: k + 1]) // sum(shares) for k in range(len(shares))]
    cuts = list(zip([0, *ends], ends))
    means = []
    for k, (low, high) in enumerate(cuts):
        rows_here = lax.optimization_barrier(lax.slice_in_dim(weights, low, high))
        means.append(mean_of_four(rows_here, first_route, second_route))

    results, updates = None, []
    for col in range(cols // width):
        *results, update = *second_mix(
            theirs[col], own[col][1], own[col][0], means[:early], scale, col,
            weights.shape, results,
        ), None
        if early < len(shares):
            *results, update = results
        updates.append(update)
    new_tracker, new_weights = results
    for k in range(early, len(shares)):
        new_weights = apply(means[k], updates, scale, cuts[k][0], cuts[early][0], weights.shape, new_weights)
    return new_weights, new_tracker


def body(weights, tracker, grad_prev, pool, out_grads, row_ids, step_index):
    levels = lax.axis_size("rep").bit_length() - 1

    def branch(level, *args):
        return two_steps(1 << level, 1 << (level + 1) % levels, *args)

    return lax.switch(
        step_index[0] % levels,
        [functools.partial(branch, level) for level in range(levels)],
        weights[0],
        tracker[0],
        grad_prev[0],
        pool[0],
        out_grads[0],
        row_ids[0],
    )


def solution(mesh):
    in_specs = (
        P("rep", "row", "col"),
        P("rep", "row", "col"),
        P("rep", "row", "col"),
        P("rep", "row", "col"),
        P("rep", None, "col", "row"),
        P("rep", None, None),
        P(),
    )
    out_specs = (P("rep", "row", "col"), P("rep", "row", "col"))
    return jax.shard_map(body, mesh=mesh, in_specs=in_specs, out_specs=out_specs, check_vma=False)
```
